32 devices in a mesh: group: 1, cent: 32 (over z, y, x, core).
Axes of the slice: x: 2, y: 2, z: 4, core: 2. Of those that a mesh axis runs over, the one named last changes fastest.
Arguments:
- embeddings: bfloat16 [12288, 768], P(('group', 'cent')), may hold values from -6 to 6
- assign: int32 [12288], P(('group', 'cent')), may hold values from 0 to 8191, as said below
- codes: int32 [12288, 96], P(('group', 'cent')), may hold values from 0 to 255
- centroids: bfloat16 [8192, 768], P(('group', 'cent')), may hold values from -6 to 6
- codebook: float32 [256, 768], P(('group', 'cent')), may hold values from -6 to 6
Outputs:
- residuals: bfloat16 [12288, 768], P(('group', 'cent'))
- new_centroids: float32 [8192, 768], P(('group', 'cent'))
- new_codebook: float32 [256, 768], P(('group', 'cent'))
The draws below stay inside these ranges and needn't reach their ends.
Inputs may be any that keep to these rules, and one draw needn't show every extreme that they name: Among the rows of one device, at most 12 have assign // 256 equal to any one value, and in every draw each device has exactly 12 rows on one such value.
All inputs are finite; a program needn't handle non-finite values.
Results may differ from the reference program's by a relative error of at most 0.001.
Values may be sent and summed in bfloat16 or wider, within the bound.
A program may use at most 128 MiB of HBM per device.

```python
import jax
import jax.numpy as jnp

D = 768
M = 96
CODEWORDS = 256
KC_DEV = 256
CAP = 12
ROWS_DEV = 384
DSUB = 8
K = 8192
ROWS = 12288
N_CENT = 32


def draw_assign(key, part):

    def one_device(sub):
        first_key, perm_key, order_key, local_key = jax.random.split(sub, 4)
        first = jax.random.randint(first_key, (), 0, min(8, N_CENT)).astype(jnp.int32)
        shuffled = jax.random.permutation(perm_key, (N_CENT - 1) * CAP)[:ROWS_DEV - CAP].astype(jnp.int32)
        label = shuffled // CAP
        others = label + (label >= first).astype(jnp.int32)
        owners = jnp.concatenate([jnp.full((CAP,), first, jnp.int32), others])
        owners = owners[jax.random.permutation(order_key, ROWS_DEV)]
        local = jax.random.randint(local_key, (ROWS_DEV,), 0, KC_DEV).astype(jnp.int32)
        return owners * KC_DEV + local
    keys = jax.random.split(jax.random.fold_in(key, 11), N_CENT)
    return jax.vmap(one_device)(keys).reshape(-1).astype(jnp.int32)


def plant(array, own_key, least, top_value):
    dims = array.shape
    spot = [jax.random.randint(jax.random.fold_in(own_key, axis), (), 0, dims[axis]) for axis in range(len(dims))]
    array = array.at[tuple(spot)].set(least)
    longest = dims.index(max(dims))
    spot[longest] = (spot[longest] + 1) % dims[longest]
    return array.at[tuple(spot)].set(top_value)


def level_of(own_key, extent, shards, least, largest):
    def one(position, blocks):
        heights = jax.random.uniform(jax.random.fold_in(jax.random.fold_in(own_key, 6), position), (blocks,), jnp.float32, least / len(shards), largest / len(shards))
        return jnp.repeat(jnp.exp(heights), extent[position] // blocks).reshape((-1,) + (1,) * (len(extent) - position - 1))

    gain = one(*shards[0])
    for cut in shards[1:]:
        gain = gain * one(*cut)
    return gain


def bell_draw(stream_key, extent, deviation, bound, cuts=(), kind=jnp.bfloat16):
    factor_of = level_of(stream_key, extent, cuts, -0.22, 0.18) if cuts else 1.0
    array = jax.random.normal(stream_key, extent, jnp.float32) * deviation * factor_of
    return jnp.minimum(jnp.maximum(array, -bound), bound).astype(kind)


def setup_inputs(seed: int = 0, part: int = 0) -> dict:
    seeds = jax.random.split(jax.random.key(seed), 6)
    part_keys = jax.random.split(jax.random.fold_in(seeds[5], part), 6)
    return {
        "embeddings": bell_draw(part_keys[0], (ROWS, D), 1.0, 6.0, ((0, 32),)),
        "assign": draw_assign(jax.random.fold_in(jax.random.fold_in(seeds[5], part), 71), part),
        "codes": plant(jax.random.randint(part_keys[2], (ROWS, M), 0, CODEWORDS), jax.random.fold_in(part_keys[2], 1), 0, CODEWORDS - 1).astype(jnp.int32),
        "centroids": bell_draw(part_keys[3], (K, D), 1.0, 6.0, ((0, 32),)),
        "codebook": bell_draw(part_keys[4], (CODEWORDS, D), 1.0, 6.0, ((0, 32),), jnp.float32),
    }


prior_weight = 16.0


def reference(embeddings, assign, codes, centroids, codebook):
    rows_f = embeddings.astype(jnp.float32)
    chosen = jnp.take(centroids, assign, axis=0).astype(jnp.float32)
    residuals = (rows_f - chosen).astype(jnp.bfloat16)
    coarse_sums = jax.ops.segment_sum(rows_f, assign, num_segments=K)
    coarse_counts = jax.ops.segment_sum(jnp.ones((ROWS,), jnp.float32), assign, num_segments=K)
    new_centroids = (coarse_sums + prior_weight * centroids.astype(jnp.float32)) / (coarse_counts[:, None] + prior_weight)
    pieces = residuals.astype(jnp.float32).reshape(ROWS * M, DSUB)
    index = (codes * M + jnp.arange(M, dtype=jnp.int32)[None, :]).reshape(-1).astype(jnp.int32)
    code_sums = jax.ops.segment_sum(pieces, index, num_segments=CODEWORDS * M).reshape(CODEWORDS, D)
    code_counts = jax.ops.segment_sum(jnp.ones((ROWS * M,), jnp.float32), index, num_segments=CODEWORDS * M).reshape(CODEWORDS, M)
    spread_counts = jnp.repeat(code_counts, DSUB, axis=1)
    new_codebook = (code_sums + prior_weight * codebook) / (spread_counts + prior_weight)
    return (residuals, new_centroids, new_codebook)
```

```python
import functools

import jax
import jax.numpy as jnp
from jax import lax
from jax.experimental import pallas as pl
from jax.experimental.pallas import tpu as pltpu
from jax.sharding import PartitionSpec as P

CAP = 12
FULL = 8
REST = CAP - FULL
LANES = 128

prior_weight = 16.0
f32 = jnp.float32
bf16 = jnp.bfloat16


def dot(a, b, ca=1, cb=0, **kw):
    return lax.dot_general(
        a, b, (((ca,), (cb,)), ((), ())), preferred_element_type=f32, **kw
    )


def step_kernel(
    peers,
    assign_any,
    emb_any,
    codes_any,
    cent_any,
    book_any,
    resid_ref,
    newc_ref,
    newb_ref,
    ids_s,
    ids_r,
    ans_s,
    ans_r,
    rows_s,
    rows_r,
    pair_s,
    pair_r,
    sum_s,
    sum_r,
    place_s,
    codes_t,
    res_t,
    sums_t,
    counts_t,
    emb_ref,
    cent_ref,
    assign_ref,
    codes_ref,
    book_ref,
    load_sem,
    send_sem,
    recv_sem,
    pair_send,
    pair_recv,
):
    me = lax.axis_index("cent")
    num_rows, width = emb_ref.shape
    half = width // 2
    subspaces = codes_ref.shape[0]
    sub_width = width // subspaces
    held = cent_ref.shape[0]
    mine = book_ref.shape[0]
    words = mine * peers
    slots = peers * FULL
    chips = peers // 2
    part = peers * 3 // 4
    core = lax.rem(me, 2)
    chip = lax.div(me, 2)
    tiles = width // LANES

    load_emb = pltpu.make_async_copy(emb_any, emb_ref, load_sem.at[0])
    load_cent = pltpu.make_async_copy(cent_any, cent_ref, load_sem.at[1])
    load_assign = pltpu.make_async_copy(assign_any, assign_ref, load_sem.at[2])
    load_codes = pltpu.make_async_copy(codes_any, codes_ref, load_sem.at[3])
    load_book = pltpu.make_async_copy(book_any, book_ref, load_sem.at[4])
    load_assign.start()
    load_emb.start()
    load_codes.start()
    load_cent.start()
    load_book.start()
    counts_t[...] = jnp.zeros_like(counts_t)
    barrier = pltpu.get_barrier_semaphore()

    def greet(d, carry):
        peer = lax.rem(me + d, peers)
        pl.semaphore_signal(barrier, inc=1, device_id={"cent": peer})
        return carry

    lax.fori_loop(1, peers, greet, 0)

    def start_own(src, dst, k, index):
        pltpu.make_async_copy(src.at[index], dst.at[index], recv_sem.at[k]).start()

    def start_sends(src, dst, k, first, last):
        def send(d, carry):
            peer = lax.rem(me + d, peers)
            pltpu.make_async_remote_copy(
                src_ref=src.at[peer],
                dst_ref=dst.at[me],
                send_sem=send_sem.at[k],
                recv_sem=recv_sem.at[k],
                device_id={"cent": peer},
            ).start()
            return carry

        lax.fori_loop(first, last, send, 0)

    def arrived(dst, k):
        pltpu.make_async_copy(dst, dst, recv_sem.at[k]).wait()

    def sent(src, k):
        part = src.at[pl.ds(0, src.shape[0] - 1)]
        pltpu.make_async_copy(part, part, send_sem.at[k]).wait()

    load_assign.wait()
    a = assign_ref[...].reshape(1, num_rows)
    peer_ids = lax.broadcasted_iota(jnp.int32, (peers, num_rows), 0)
    low = peer_ids * held
    hits = ((a >= low) & (a < low + held)).astype(f32)
    before = (
        lax.broadcasted_iota(jnp.int32, (num_rows, num_rows), 0)
        < lax.broadcasted_iota(jnp.int32, (num_rows, num_rows), 1)
    ).astype(f32).astype(bf16)
    earlier = dot(hits.astype(bf16), before)
    rank = jnp.sum(earlier * hits, axis=0, keepdims=True).astype(jnp.int32)
    owner = jnp.sum(peer_ids.astype(f32) * hits, axis=0, keepdims=True).astype(jnp.int32)
    label = (a - owner * held + 1).astype(f32)
    labels = jnp.broadcast_to(label, (LANES, num_rows)).astype(bf16)
    slot_ids = lax.broadcasted_iota(jnp.int32, (slots, num_rows), 0)
    base = owner * FULL + rank
    late = rank >= FULL
    targets = (
        jnp.where(late, -1, base),
        jnp.where(late, base - FULL, -1),
        jnp.where(late, base - (FULL - REST), -1),
    )
    places = [(slot_ids == target).astype(f32).astype(bf16) for target in targets]
    for i in range(3):
        place_s[i] = places[i]
    ids_s[:, :, :LANES] = dot(places[0], labels, 1, 1).astype(bf16).reshape(peers, FULL, LANES)
    ids_s[:, :, LANES:] = (
        dot(places[1] + places[2], labels, 1, 1).astype(bf16).reshape(peers, FULL, LANES)
    )

    pl.semaphore_wait(barrier, peers - 1)
    start_own(ids_s, ids_r, 0, me)
    start_sends(ids_s, ids_r, 0, 1, peers)

    load_emb.wait()
    emb = emb_ref[...]
    rows_s[:, :, :width] = dot(places[0], emb).astype(bf16).reshape(peers, FULL, width)
    rows_s[:, :, width:] = (
        (dot(places[1], emb[:, :half]) + dot(places[2], emb[:, half:]))
        .astype(bf16)
        .reshape(peers, FULL, half)
    )
    start_own(rows_s, rows_r, 2, me)
    load_codes.wait()
    shifted = (codes_ref[...] + 1).astype(f32).astype(bf16)
    lower = lax.broadcasted_iota(jnp.int32, (subspaces, slots), 0) < subspaces // 2
    codes_t[:, :slots] = dot(shifted, places[0], 1, 1)
    codes_t[:, slots:] = jnp.where(
        lower, dot(shifted, places[1], 1, 1), dot(shifted, places[2], 1, 1)
    )

    arrived(ids_r, 0)
    lane = lax.broadcasted_iota(jnp.int32, (slots, LANES), 1).astype(f32)

    def pick_of(got):
        got = got.reshape(slots, LANES).astype(f32)
        return jnp.concatenate(
            [
                (got == lane + (1.0 + LANES * i)).astype(f32).astype(bf16)
                for i in range(held // LANES)
            ],
            axis=1,
        )

    pick_a = pick_of(ids_r[:, :, :LANES])
    got_b = ids_r[:, :, LANES:]
    front = lax.broadcasted_iota(jnp.int32, got_b.shape, 1) < REST
    pick_b = pick_of(jnp.where(front, got_b.astype(f32), 0.0))
    pick_c = pick_of(jnp.where(front, 0.0, got_b.astype(f32)))
    load_cent.wait()
    cent = cent_ref[...]
    ans_s[:, :, :width] = dot(pick_a, cent).astype(bf16).reshape(peers, FULL, width)
    ans_s[:, :, width:] = (
        (dot(pick_b, cent[:, :half]) + dot(pick_c, cent[:, half:]))
        .astype(bf16)
        .reshape(peers, FULL, half)
    )
    start_own(ans_s, ans_r, 1, me)
    start_sends(ans_s, ans_r, 1, 1, peers)
    start_sends(rows_s, rows_r, 2, 1, part)

    arrived(ans_r, 1)
    res = (
        rows_s[...].reshape(slots, width + half).astype(f32)
        - ans_r[...].reshape(slots, width + half).astype(f32)
    )
    res_t[...] = res.T
    res = res.astype(bf16)

    per = LANES // sub_width
    word = (lax.broadcasted_iota(jnp.int32, (words, 2 * slots), 0) + 1).astype(f32).astype(bf16)
    ones = jnp.ones((2 * slots, LANES), bf16)
    plain = jnp.ones((sub_width, 2 * slots), f32)

    def pair_copy(t):
        return pltpu.make_async_remote_copy(
            src_ref=pair_s.at[t, 1 - core],
            dst_ref=pair_r.at[t],
            send_sem=pair_send.at[t],
            recv_sem=pair_recv.at[t],
            device_id={"cent": me + 1 - 2 * core},
        )

    def put(t, value):
        if mine % 8 == 0:
            split = value.reshape(chips, 2, mine, LANES)
            for c in range(2):
                pair_s[t, c] = split[:, c]
        else:
            for p in range(peers):
                pair_s[t, p % 2, p // 2] = value[p * mine : (p + 1) * mine]
        pair_copy(t).start()

    for t in range(tiles):

        def one(u, carry, t=t):
            m = t * per + u
            at = pl.multiple_of(m * sub_width, sub_width)
            beside = pl.multiple_of(width + t * LANES % half + u * sub_width, sub_width)
            part = jnp.concatenate(
                [res_t[pl.ds(at, sub_width), :], res_t[pl.ds(beside, sub_width), :]], axis=1
            )
            lhs = jnp.concatenate([part, plain], axis=0).astype(bf16)
            code = jnp.broadcast_to(codes_t[pl.ds(m, 1), :], (words, 2 * slots)).astype(bf16)
            onehot = jnp.where(code == word, jnp.ones_like(word), jnp.zeros_like(word))
            prod = dot(lhs, onehot, 1, 1)
            sums_t[pl.ds(at, sub_width), :] = prod[:sub_width]
            counts_t[pl.ds(m, 1), :] = prod[sub_width : sub_width + 1]
            return carry

        lax.fori_loop(0, per, one, 0, unroll=16)
        put(t, sums_t[t * LANES : (t + 1) * LANES, :].T)
    put(tiles, counts_t[...].T)

    for t in range(tiles + 1):
        pair_copy(t).wait_recv()
        sum_s[:, :, t * LANES : (t + 1) * LANES] = pair_s[t, core] + pair_r[t]
    start_own(sum_s, sum_r, 3, chip)

    def send_sum(d, carry):
        other = lax.rem(chip + d, chips)
        pltpu.make_async_remote_copy(
            src_ref=sum_s.at[other],
            dst_ref=sum_r.at[chip],
            send_sem=send_sem.at[3],
            recv_sem=recv_sem.at[3],
            device_id={"cent": other * 2 + core},
        ).start()
        return carry

    lax.fori_loop(1, chips, send_sum, 0)

    start_sends(rows_s, rows_r, 2, part, peers)
    for i in range(2):
        at = slice(i * half, (i + 1) * half)
        resid_ref[:, at] = (
            dot(place_s[0], res[:, at], 0, 0) + dot(place_s[1 + i], res[:, width:], 0, 0)
        ).astype(bf16)
    arrived(rows_r, 2)
    held_counts = dot(pick_a, ones[:slots], 0, 0) + dot(pick_b, ones[:slots], 0, 0) + prior_weight
    rest = rows_r[:, :, width:].reshape(slots, half)
    main = rows_r[:, :, :width].reshape(slots, width)
    for i, pick in enumerate((pick_b, pick_c)):
        coarse = dot(pick_a, main[:, i * half : (i + 1) * half], 0, 0) + dot(pick, rest, 0, 0)
        for t in range(half // LANES):
            cut = slice(t * LANES, (t + 1) * LANES)
            at = slice(i * half + t * LANES, i * half + (t + 1) * LANES)
            newc_ref[:, at] = (
                coarse[:, cut] + prior_weight * cent_ref[:, at].astype(f32)
            ) / held_counts

    arrived(sum_r, 3)
    totals = jnp.sum(sum_r[...], axis=0)
    col = lax.broadcasted_iota(jnp.int32, (LANES, width), 1)
    row = lax.broadcasted_iota(jnp.int32, (LANES, width), 0) * sub_width
    expand = ((col >= row) & (col < row + sub_width)).astype(f32)
    spread = dot(totals[:, width:], expand, precision=lax.Precision.HIGHEST)
    load_book.wait()
    newb_ref[...] = (totals[:, :width] + prior_weight * book_ref[...]) / (spread + prior_weight)
    sent(ids_s, 0)
    sent(ans_s, 1)
    sent(rows_s, 2)
    sent(sum_s, 3)
    for t in range(tiles + 1):
        pair_copy(t).wait_send()


def store_kernel(*refs):
    copies = [
        pltpu.make_async_copy(refs[i], refs[3 + i], refs[6].at[i]) for i in range(3)
    ]
    for copy in copies:
        copy.start()
    for copy in copies:
        copy.wait()


def shards(embeddings, assign, codes, centroids, codebook):
    num_rows, width = embeddings.shape
    held = centroids.shape[0]
    mine = codebook.shape[0]
    subspaces = codes.shape[1]
    peers = lax.axis_size("cent")
    slots = peers * FULL
    long = width + width // 2
    tiles = width // LANES + 1
    hbm = pl.BlockSpec(memory_space=pltpu.HBM)
    vmem = pl.BlockSpec(memory_space=pltpu.VMEM)
    outs = (
        jax.ShapeDtypeStruct((num_rows, width), bf16),
        jax.ShapeDtypeStruct((held, width), f32),
        jax.ShapeDtypeStruct((mine, width), f32),
    )
    made = pl.pallas_call(
        functools.partial(step_kernel, peers),
        out_shape=tuple(pltpu.VMEM(out.shape, out.dtype) for out in outs),
        in_specs=[hbm] * 5,
        out_specs=(vmem,) * 3,
        scratch_shapes=[
            pltpu.VMEM((peers, FULL, 2 * LANES), bf16),
            pltpu.VMEM((peers, FULL, 2 * LANES), bf16),
            pltpu.VMEM((peers, FULL, long), bf16),
            pltpu.VMEM((peers, FULL, long), bf16),
            pltpu.VMEM((peers, FULL, long), bf16),
            pltpu.VMEM((peers, FULL, long), bf16),
            pltpu.VMEM((tiles, 2, peers // 2, mine, LANES), f32),
            pltpu.VMEM((tiles, peers // 2, mine, LANES), f32),
            pltpu.VMEM((peers // 2, mine, width + LANES), f32),
            pltpu.VMEM((peers // 2, mine, width + LANES), f32),
            pltpu.VMEM((3, slots, num_rows), bf16),
            pltpu.VMEM((subspaces, 2 * slots), f32),
            pltpu.VMEM((long, slots), f32),
            pltpu.VMEM((width, mine * peers), f32),
            pltpu.VMEM((LANES, mine * peers), f32),
            pltpu.VMEM((num_rows, width), bf16),
            pltpu.VMEM((held, width), bf16),
            pltpu.VMEM((num_rows,), jnp.int32),
            pltpu.VMEM((subspaces, num_rows), jnp.int32),
            pltpu.VMEM((mine, width), f32),
            pltpu.SemaphoreType.DMA((5,)),
            pltpu.SemaphoreType.DMA((4,)),
            pltpu.SemaphoreType.DMA((4,)),
            pltpu.SemaphoreType.DMA((tiles,)),
            pltpu.SemaphoreType.DMA((tiles,)),
        ],
        compiler_params=pltpu.CompilerParams(
            collective_id=0, has_side_effects=True, vmem_limit_bytes=48 * 1024 * 1024
        ),
    )(
        *(
            pltpu.with_memory_space_constraint(x, pltpu.HBM)
            for x in (assign, embeddings, codes.T, centroids, codebook)
        )
    )
    return pl.pallas_call(
        store_kernel,
        out_shape=outs,
        in_specs=[vmem] * 3,
        out_specs=(hbm,) * 3,
        scratch_shapes=[pltpu.SemaphoreType.DMA((3,))],
    )(*(pltpu.with_memory_space_constraint(x, pltpu.VMEM) for x in made))


def solution(mesh):
    spec = P(("group", "cent"), None)
    in_specs = (spec, P(("group", "cent")), spec, spec, spec)
    return jax.shard_map(
        shards, mesh=mesh, in_specs=in_specs, out_specs=(spec, spec, spec), check_vma=False
    )
```

```python
import functools

import jax
import jax.numpy as jnp
from jax import lax
from jax.experimental import pallas as pl
from jax.experimental.pallas import tpu as pltpu
from jax.sharding import PartitionSpec as P

CAP = 12
FULL = 8
REST = CAP - FULL
LANES = 128
INNER = 4
CHUNKS = 3
AHEAD = 9

prior_weight = 16.0
f32 = jnp.float32
bf16 = jnp.bfloat16


def dot(a, b, ca=1, cb=0, **kw):
    return lax.dot_general(
        a, b, (((ca,), (cb,)), ((), ())), preferred_element_type=f32, **kw
    )


def send_plan(peers):
    eighth = peers // 8
    cuts = [(1, 4 * eighth), (4 * eighth, peers)]
    rows = [(1, 2 * eighth), (2 * eighth, 4 * eighth), (4 * eighth, 6 * eighth), (6 * eighth, peers)]
    plan = [(None,) + cut for cut in rows[:1]]
    for c in range(CHUNKS):
        plan += [(c,) + cut for cut in cuts]
    return plan + [(None,) + cut for cut in rows[1:]]


def step_kernel(
    peers,
    assign_any,
    emb_any,
    codes_any,
    cent_any,
    book_any,
    resid_ref,
    newc_ref,
    newb_ref,
    ids_s,
    ids_r,
    ans_s,
    ans_r,
    rows_s,
    rows_r,
    pair_s,
    pair_r,
    plane_s,
    plane_r,
    line_s,
    line_r,
    place_s,
    pick_s,
    pick_t,
    codes_c,
    onehot,
    res_s,
    res_t,
    sums_t,
    counts_t,
    base_s,
    emb_ref,
    cent_ref,
    assign_ref,
    codes_ref,
    book_ref,
    load_sem,
    ids_sem,
    send_sem,
    recv_sem,
    pair_send,
    pair_recv,
    plane_send,
    plane_recv,
    line_send,
    line_recv,
):
    me = lax.axis_index("cent")
    num_rows, width = emb_ref.shape
    side = width // 2
    subspaces = codes_ref.shape[0]
    sub_width = width // subspaces
    held = cent_ref.shape[0]
    mine = book_ref.shape[0]
    words = mine * peers
    slots = peers * FULL
    half = peers // 2
    core = lax.rem(me, 2)
    outer = peers // 2 // INNER
    tiles = width // LANES
    bits = peers.bit_length() - 1
    span = 3 * LANES
    plan = send_plan(peers)

    move = [(1 - 2 * lax.rem(lax.div(me, 1 << i), 2)) * (1 << i) for i in range(bits)]
    turn = [move[-1]] + move[:-1]

    def peer_of(p):
        peer = me
        for i in range(bits):
            peer = peer + lax.rem(lax.div(p, 1 << i), 2) * turn[i]
        return peer

    def away(d):
        return me + sum(move[i] for i in range(bits) if d >> i & 1)

    load_assign = pltpu.make_async_copy(assign_any, assign_ref, load_sem.at[0])
    load_emb = pltpu.make_async_copy(emb_any, emb_ref, load_sem.at[1])
    load_cent = pltpu.make_async_copy(cent_any, cent_ref, load_sem.at[2])
    load_codes = pltpu.make_async_copy(codes_any, codes_ref, load_sem.at[3])
    load_book = pltpu.make_async_copy(book_any, book_ref, load_sem.at[4])
    load_assign.start()
    load_emb.start()
    load_cent.start()
    load_codes.start()
    load_book.start()
    barrier = pltpu.get_barrier_semaphore()

    def greet(d, carry):
        pl.semaphore_signal(barrier, inc=1, device_id={"cent": lax.rem(me + d, peers)})
        return carry

    lax.fori_loop(1, peers, greet, 0)

    def each_peer(first, last, copy):
        def send(p, carry):
            copy(p, peer_of(p)).start()
            return carry

        lax.fori_loop(first, last, send, 0)

    def ids_copy(p, peer):
        return pltpu.make_async_remote_copy(
            src_ref=ids_s.at[p],
            dst_ref=ids_r.at[p],
            send_sem=ids_sem.at[0],
            recv_sem=ids_sem.at[1],
            device_id={"cent": peer},
        )

    def piece_of(k, rows, answers, at):
        c = plan[k][0]
        if c is None:
            return rows.at[at]
        return answers.at[at, :, pl.ds(c * span, span)]

    def issue(k):
        if k >= AHEAD:
            sent(k - AHEAD)

        def copy(p, peer):
            return pltpu.make_async_remote_copy(
                src_ref=piece_of(k, rows_s, ans_s, p),
                dst_ref=piece_of(k, rows_r, ans_r, p),
                send_sem=send_sem.at[k],
                recv_sem=recv_sem.at[k],
                device_id={"cent": peer},
            )

        each_peer(plan[k][1], plan[k][2], copy)

    def wait_for(piece, sem):
        pltpu.make_async_copy(piece, piece, sem).wait()

    def sent(k):
        at = pl.ds(plan[k][1], plan[k][2] - plan[k][1])
        wait_for(piece_of(k, rows_s, ans_s, at), send_sem.at[k])

    def arrived(k):
        at = pl.ds(plan[k][1], plan[k][2] - plan[k][1])
        wait_for(piece_of(k, rows_r, ans_r, at), recv_sem.at[k])

    load_assign.wait()
    a = assign_ref[...].reshape(1, num_rows)
    slot_ids = lax.broadcasted_iota(jnp.int32, (peers, num_rows), 0)
    low = jnp.bitwise_xor((slot_ids & 1) * half + (slot_ids >> 1), me) * held
    hits = ((a >= low) & (a < low + held)).astype(f32)
    before = (
        lax.broadcasted_iota(jnp.int32, (num_rows, num_rows), 0)
        < lax.broadcasted_iota(jnp.int32, (num_rows, num_rows), 1)
    ).astype(f32).astype(bf16)
    earlier = dot(hits.astype(bf16), before)
    rank = jnp.sum(earlier * hits, axis=0, keepdims=True).astype(jnp.int32)
    position = jnp.sum(slot_ids.astype(f32) * hits, axis=0, keepdims=True).astype(jnp.int32)
    labels = (hits * (a - low + 1).astype(f32)).astype(bf16)
    ranks = (lax.broadcasted_iota(jnp.int32, (LANES, num_rows), 0) == rank).astype(f32).astype(bf16)
    ids_s[...] = dot(labels, ranks, 1, 1).reshape(peers, 1, LANES)

    pl.semaphore_wait(barrier, peers - 1)
    each_peer(1, peers, ids_copy)
    ids_r[0] = ids_s[0]

    base = position * FULL + rank
    late = rank >= FULL
    targets = (
        jnp.where(late, -1, base),
        jnp.where(late, base - FULL, -1),
        jnp.where(late, base - (FULL - REST), -1),
    )
    place_ids = lax.broadcasted_iota(jnp.int32, (slots, num_rows), 0)
    for i, target in enumerate(targets):
        place_s[i] = (place_ids == target).astype(f32).astype(bf16)

    def tile(t):
        return slice(t * LANES, (t + 1) * LANES)

    def gather(choose, table, at, out, chunks):
        n = at.stop - at.start
        for c in chunks:
            for i, value in enumerate(
                (
                    dot(choose[0, at], table[:, tile(c)]),
                    dot(choose[0, at], table[:, tile(c + CHUNKS)]),
                    dot(choose[1, at], table[:, tile(c)])
                    + dot(choose[2, at], table[:, tile(c + CHUNKS)]),
                )
            ):
                out[at.start // FULL : at.stop // FULL, :, tile(3 * c + i)] = value.astype(
                    bf16
                ).reshape(n // FULL, FULL, LANES)

    load_emb.wait()
    gather(place_s, emb_ref, slice(0, slots), rows_s, range(CHUNKS))
    issue(0)

    wait_for(ids_r.at[pl.ds(1, peers - 1)], ids_sem.at[1])
    shape = (peers, FULL, LANES)
    got = jnp.broadcast_to(ids_r[...], shape)
    lane = lax.broadcasted_iota(jnp.int32, shape, 2)
    sub = lax.broadcasted_iota(jnp.int32, shape, 1)
    front = sub < REST
    first_at = jnp.where(lane == sub, got, 0.0)
    rest_at = jnp.where(lane == jnp.where(front, sub + FULL, sub + (FULL - REST)), got, 0.0)
    label_a = jnp.sum(first_at, axis=2, keepdims=True)
    label_r = jnp.sum(rest_at, axis=2, keepdims=True)
    label_b = jnp.where(front[:, :, :1], label_r, 0.0)
    label_c = jnp.where(front[:, :, :1], 0.0, label_r)
    lane_f = lane.astype(f32)
    for i, label in enumerate((label_a, label_b, label_c)):
        for h in range(held // LANES):
            pick_s[i, :, tile(h)] = (
                (label == lane_f + (1.0 + LANES * h)).astype(f32).reshape(slots, LANES).astype(bf16)
            )
    load_cent.wait()

    gather(pick_s, cent_ref, slice(0, slots), ans_s, (0,))
    issue(1)
    issue(2)
    gather(pick_s, cent_ref, slice(0, slots), ans_s, range(1, CHUNKS))
    ans_r[0] = ans_s[0]
    rows_r[0] = rows_s[0]

    load_codes.wait()
    shifted = (codes_ref[...] + 1).astype(f32).astype(bf16)
    part = subspaces // 2
    for i in range(2):
        codes_c[i, :, :part] = dot(place_s[0], shifted[i * part : (i + 1) * part], 1, 1)
    codes_c[2, :, :part] = dot(place_s[1], shifted[:part], 1, 1) + dot(
        place_s[2], shifted[part:], 1, 1
    )

    per = LANES // sub_width
    column = (lax.broadcasted_iota(jnp.int32, (slots, LANES), 1) + 1).astype(f32)
    columns = [(column + LANES * i).astype(bf16) for i in range(words // LANES)]
    kind = lax.broadcasted_iota(jnp.int32, (16, slots), 0)
    early = lax.rem(lax.broadcasted_iota(jnp.int32, (16, slots), 1), FULL) < REST
    counted = jnp.where(kind == 0, 1.0, jnp.where((kind == 1) == early, 1.0, 0.0)).astype(bf16)
    counts_t[subspaces:] = jnp.zeros_like(counts_t[subspaces:])

    def build_onehot(c):
        def build(i, carry):
            for j in range(per):
                code = jnp.broadcast_to(
                    codes_c[i, :, c * per + j : c * per + j + 1], (slots, LANES)
                ).astype(bf16)
                at = i * part + c * per + j
                for h, value in enumerate(columns):
                    onehot[at, :, tile(h)] = jnp.where(
                        code == value, jnp.ones_like(value), jnp.zeros_like(value)
                    )
            return carry

        lax.fori_loop(0, 3, build, 0)

        def count(u, carry):
            m = c * per + u
            late_counts = dot(counted, onehot[2 * part + m])
            for i in range(2):
                counts_t[pl.ds(i * part + m, 1), :] = (
                    dot(counted, onehot[i * part + m])[:1] + late_counts[1 + i : 2 + i]
                )
            return carry

        lax.fori_loop(0, per, count, 0, unroll=4)

    front_lanes = lax.rem(lax.broadcasted_iota(jnp.int32, (sub_width, slots), 1), FULL) < REST

    def sum_chunk(c):
        cut = slice(c * span, (c + 1) * span)
        res = rows_s[:, :, cut].reshape(slots, span).astype(f32) - ans_r[:, :, cut].reshape(
            slots, span
        ).astype(f32)
        res_t[...] = res.T
        res_s[:, cut] = res.astype(bf16)

        def one(u, carry):
            m = c * per + u
            at = [pl.multiple_of(i * LANES + u * sub_width, sub_width) for i in range(3)]
            main = [res_t[pl.ds(at[i], sub_width), :].astype(bf16) for i in range(2)]
            beside = res_t[pl.ds(at[2], sub_width), :]
            both = jnp.concatenate(
                [jnp.where(front_lanes, beside, 0.0), jnp.where(front_lanes, 0.0, beside)], axis=0
            ).astype(bf16)
            late_sums = dot(both, onehot[2 * part + m])
            for i in range(2):
                sums_t[pl.ds(at[i], sub_width), :] = (
                    dot(main[i], onehot[i * part + m])
                    + late_sums[i * sub_width : (i + 1) * sub_width]
                )
            return carry

        lax.fori_loop(0, per, one, 0, unroll=8)

    cuts = [(2 * c + (c > 1), 2 * c + 2 + (c > 0)) for c in range(CHUNKS)]
    order = []
    for c in range(CHUNKS):
        order += [c, c + CHUNKS] + ([tiles] if c == 1 else [])

    def pair_copy(c):
        at = pl.ds(cuts[c][0], cuts[c][1] - cuts[c][0])
        return pltpu.make_async_remote_copy(
            src_ref=pair_s.at[1 - core, at],
            dst_ref=pair_r.at[at],
            send_sem=pair_send.at[c],
            recv_sem=pair_recv.at[c],
            device_id={"cent": away(1)},
        )

    def put(c):
        for k in range(*cuts[c]):
            t = order[k]
            value = (counts_t[...] if t == tiles else sums_t[tile(t // CHUNKS), :]).T
            if mine % 8 == 0:
                split = value.reshape(outer, INNER, 2, mine, LANES)
                for b in range(2):
                    for i in range(INNER):
                        pair_s[b, k, i] = split[:, i, b]
            else:
                for p in range(peers):
                    pair_s[p % 2, k, p // 2 % INNER, p // 2 // INNER] = value[
                        p * mine : (p + 1) * mine
                    ]
        pair_copy(c).start()

    def hops(src, dst, sems, c, count, stride, place):
        at = pl.ds(cuts[c][0], cuts[c][1] - cuts[c][0])
        for e in range(1, count):
            peer = away(stride * e)
            pltpu.make_async_remote_copy(
                src_ref=src.at[place(peer), at],
                dst_ref=dst.at[e - 1, at],
                send_sem=sems[0].at[c],
                recv_sem=sems[1].at[c],
                device_id={"cent": peer},
            ).start()

    def hops_wait(dst, sem, c, count):
        at = pl.ds(cuts[c][0], cuts[c][1] - cuts[c][0])
        wait_for(dst.at[pl.ds(0, count - 1), at], sem.at[c])

    def inner_of(peer):
        return lax.rem(lax.div(peer, 2), INNER)

    def outer_of(peer):
        return lax.div(peer, 2 * INNER)

    def add_pair(c):
        pair_copy(c).wait_recv()
        for k in range(*cuts[c]):
            plane_s[:, k] = pair_s[core, k] + pair_r[k]
        hops(plane_s, plane_r, (plane_send, plane_recv), c, INNER, 2, inner_of)

    def add_plane(c):
        first, last = cuts[c]
        hops_wait(plane_r, plane_recv, c, INNER)
        total = plane_s[inner_of(me), first:last]
        for e in range(1, INNER):
            total = total + plane_r[e - 1, first:last]
        for o in range(outer):
            line_s[o, first:last] = total[:, o]
        hops(line_s, line_r, (line_send, line_recv), c, outer, 2 * INNER, outer_of)

    ones = jnp.ones((slots, LANES), bf16)
    tail = slice(plan[-1][1] * FULL, slots)
    lead = slice(0, plan[-1][1] * FULL)

    issue(3)
    issue(4)
    issue(5)
    issue(6)
    issue(7)
    issue(8)
    issue(9)
    build_onehot(0)
    build_onehot(1)
    build_onehot(2)
    arrived(1)
    arrived(2)
    sum_chunk(0)
    put(0)
    add_pair(0)
    weights = dot(pick_s[0], ones, 0, 0) + dot(pick_s[1], ones, 0, 0) + prior_weight
    inverse = 1.0 / weights
    for i in range(2):
        pick_t[i] = jnp.concatenate([pick_s[0, tail], pick_s[1 + i, tail]], axis=0).T
    arrived(3)
    arrived(4)
    sum_chunk(1)
    put(1)
    add_pair(1)
    add_plane(0)
    arrived(5)
    arrived(6)
    sum_chunk(2)
    put(2)
    add_pair(2)
    add_plane(1)
    for c in range(CHUNKS):
        for i in range(2):
            resid_ref[:, tile(c + CHUNKS * i)] = (
                dot(place_s[0], res_s[:, tile(3 * c + i)], 0, 0)
                + dot(place_s[1 + i], res_s[:, tile(3 * c + 2)], 0, 0)
            ).astype(bf16)
    add_plane(2)

    def coarse(at, choose):
        out = []
        for i in range(2):
            for c in range(CHUNKS):
                main = rows_r[at.start // FULL : at.stop // FULL, :, tile(3 * c + i)]
                rest = rows_r[at.start // FULL : at.stop // FULL, :, tile(3 * c + 2)]
                n = at.stop - at.start
                out.append((tile(c + CHUNKS * i), choose(i, main.reshape(n, LANES), rest.reshape(n, LANES))))
        return out

    arrived(0)
    arrived(7)
    arrived(8)
    for cols, value in coarse(
        lead,
        lambda i, main, rest: dot(pick_s[0, lead], main, 0, 0) + dot(pick_s[1 + i, lead], rest, 0, 0),
    ):
        base_s[:, cols] = value + prior_weight * cent_ref[:, cols].astype(f32)
    load_book.wait()
    col = lax.broadcasted_iota(jnp.int32, (LANES, width), 1)
    row = lax.broadcasted_iota(jnp.int32, (LANES, width), 0) * sub_width
    expand = ((col >= row) & (col < row + sub_width)).astype(f32)
    for c in range(CHUNKS):
        hops_wait(line_r, line_recv, c, outer)
    own = line_s[outer_of(me)]
    for e in range(1, outer):
        own = own + line_r[e - 1]
    spread = dot(own[order.index(tiles)], expand, precision=lax.Precision.HIGHEST)
    for t in range(tiles):
        newb_ref[:, tile(t)] = (own[order.index(t)] + prior_weight * book_ref[:, tile(t)]) / (
            spread[:, tile(t)] + prior_weight
        )

    arrived(9)
    for cols, value in coarse(
        tail, lambda i, main, rest: dot(pick_t[i], jnp.concatenate([main, rest], axis=0))
    ):
        newc_ref[:, cols] = (value + base_s[:, cols]) * inverse

    wait_for(ids_s.at[pl.ds(1, peers - 1)], ids_sem.at[0])
    for k in range(len(plan) - AHEAD, len(plan)):
        sent(k)
    for c in range(CHUNKS):
        pair_copy(c).wait_send()
        hops_wait(plane_r, plane_send, c, INNER)
        hops_wait(line_r, line_send, c, outer)


def store_kernel(*refs):
    copies = [
        pltpu.make_async_copy(refs[i], refs[3 + i], refs[6].at[i]) for i in range(3)
    ]
    for copy in copies:
        copy.start()
    for copy in copies:
        copy.wait()


def shards(embeddings, assign, codes, centroids, codebook):
    num_rows, width = embeddings.shape
    held = centroids.shape[0]
    mine = codebook.shape[0]
    subspaces = codes.shape[1]
    peers = lax.axis_size("cent")
    slots = peers * FULL
    words = mine * peers
    outer = peers // 2 // INNER
    long = width + width // 2
    tiles = width // LANES + 1
    plan = send_plan(peers)
    last = (peers - plan[-1][1]) * FULL
    hbm = pl.BlockSpec(memory_space=pltpu.HBM)
    vmem = pl.BlockSpec(memory_space=pltpu.VMEM)
    outs = (
        jax.ShapeDtypeStruct((num_rows, width), bf16),
        jax.ShapeDtypeStruct((held, width), f32),
        jax.ShapeDtypeStruct((mine, width), f32),
    )
    made = pl.pallas_call(
        functools.partial(step_kernel, peers),
        out_shape=tuple(pltpu.VMEM(out.shape, out.dtype) for out in outs),
        in_specs=[hbm] * 5,
        out_specs=(vmem,) * 3,
        scratch_shapes=[
            pltpu.VMEM((peers, 1, LANES), f32),
            pltpu.VMEM((peers, 1, LANES), f32),
            pltpu.VMEM((peers, FULL, long), bf16),
            pltpu.VMEM((peers, FULL, long), bf16),
            pltpu.VMEM((peers, FULL, long), bf16),
            pltpu.VMEM((peers, FULL, long), bf16),
            pltpu.VMEM((2, tiles, INNER, outer, mine, LANES), f32),
            pltpu.VMEM((tiles, INNER, outer, mine, LANES), f32),
            pltpu.VMEM((INNER, tiles, outer, mine, LANES), f32),
            pltpu.VMEM((INNER - 1, tiles, outer, mine, LANES), f32),
            pltpu.VMEM((outer, tiles, mine, LANES), f32),
            pltpu.VMEM((outer - 1, tiles, mine, LANES), f32),
            pltpu.VMEM((3, slots, num_rows), bf16),
            pltpu.VMEM((3, slots, held), bf16),
            pltpu.VMEM((2, held, 2 * last), bf16),
            pltpu.VMEM((3, slots, LANES), f32),
            pltpu.VMEM((subspaces * 3 // 2, slots, words), bf16),
            pltpu.VMEM((slots, long), bf16),
            pltpu.VMEM((3 * LANES, slots), f32),
            pltpu.VMEM((2 * LANES, words), f32),
            pltpu.VMEM((LANES, words), f32),
            pltpu.VMEM((held, width), f32),
            pltpu.VMEM((num_rows, width), bf16),
            pltpu.VMEM((held, width), bf16),
            pltpu.VMEM((num_rows,), jnp.int32),
            pltpu.VMEM((subspaces, num_rows), jnp.int32),
            pltpu.VMEM((mine, width), f32),
            pltpu.SemaphoreType.DMA((5,)),
            pltpu.SemaphoreType.DMA((2,)),
            pltpu.SemaphoreType.DMA((len(plan),)),
            pltpu.SemaphoreType.DMA((len(plan),)),
        ]
        + [pltpu.SemaphoreType.DMA((CHUNKS,))] * 6,
        compiler_params=pltpu.CompilerParams(
            collective_id=0, has_side_effects=True, vmem_limit_bytes=56 * 1024 * 1024
        ),
    )(
        *(
            pltpu.with_memory_space_constraint(x, pltpu.HBM)
            for x in (assign, embeddings, codes.T, centroids, codebook)
        )
    )
    return pl.pallas_call(
        store_kernel,
        out_shape=outs,
        in_specs=[vmem] * 3,
        out_specs=(hbm,) * 3,
        scratch_shapes=[pltpu.SemaphoreType.DMA((3,))],
    )(*(pltpu.with_memory_space_constraint(x, pltpu.VMEM) for x in made))


def solution(mesh):
    spec = P(("group", "cent"), None)
    in_specs = (spec, P(("group", "cent")), spec, spec, spec)
    return jax.shard_map(
        shards, mesh=mesh, in_specs=in_specs, out_specs=(spec, spec, spec), check_vma=False
    )
```

```python
import functools

import jax
import jax.numpy as jnp
from jax import lax
from jax.experimental import pallas as pl
from jax.experimental.pallas import tpu as pltpu
from jax.sharding import PartitionSpec as P

CAP = 12
FULL = 8
REST = CAP - FULL
LANES = 128
INNER = 4
CHUNKS = 3
DIRECT = (2,)
AHEAD = 10

prior_weight = 16.0
f32 = jnp.float32
bf16 = jnp.bfloat16


def dot(a, b, ca=1, cb=0, **kw):
    return lax.dot_general(
        a, b, (((ca,), (cb,)), ((), ())), preferred_element_type=f32, **kw
    )


def send_plan(peers):
    eighth = peers // 8
    cuts = [(1, 4 * eighth), (4 * eighth, peers)]
    rows = [(1, 2 * eighth), (2 * eighth, 4 * eighth), (4 * eighth, 6 * eighth), (6 * eighth, peers)]
    plan = [(None,) + cut for cut in rows[:1]]
    for c in range(CHUNKS):
        plan += [(c,) + cut for cut in cuts]
    return plan + [(None,) + cut for cut in rows[1:]]


def step_kernel(
    peers,
    assign_any,
    emb_any,
    codes_any,
    cent_any,
    book_any,
    resid_ref,
    newc_ref,
    newb_ref,
    ids_s,
    ids_r,
    ans_s,
    ans_r,
    rows_s,
    rows_r,
    pair_s,
    pair_r,
    plane_s,
    plane_r,
    line_s,
    line_r,
    direct_r,
    place_s,
    pick_s,
    pick_t,
    codes_c,
    onehot,
    res_s,
    res_t,
    sums_t,
    counts_t,
    base_s,
    emb_ref,
    cent_ref,
    assign_ref,
    codes_ref,
    book_ref,
    load_sem,
    ids_sem,
    send_sem,
    recv_sem,
    pair_send,
    pair_recv,
    plane_send,
    plane_recv,
    line_send,
    line_recv,
):
    me = lax.axis_index("cent")
    num_rows, width = emb_ref.shape
    side = width // 2
    subspaces = codes_ref.shape[0]
    sub_width = width // subspaces
    held = cent_ref.shape[0]
    mine = book_ref.shape[0]
    words = mine * peers
    slots = peers * FULL
    half = peers // 2
    core = lax.rem(me, 2)
    outer = peers // 2 // INNER
    tiles = width // LANES
    bits = peers.bit_length() - 1
    span = 3 * LANES
    plan = send_plan(peers)

    move = [(1 - 2 * lax.rem(lax.div(me, 1 << i), 2)) * (1 << i) for i in range(bits)]
    turn = [move[-1]] + move[:-1]

    def peer_of(p):
        peer = me
        for i in range(bits):
            peer = peer + lax.rem(lax.div(p, 1 << i), 2) * turn[i]
        return peer

    def away(d):
        return me + sum(move[i] for i in range(bits) if d >> i & 1)

    load_assign = pltpu.make_async_copy(assign_any, assign_ref, load_sem.at[0])
    load_emb = pltpu.make_async_copy(emb_any, emb_ref, load_sem.at[1])
    load_cent = pltpu.make_async_copy(cent_any, cent_ref, load_sem.at[2])
    load_codes = pltpu.make_async_copy(codes_any, codes_ref, load_sem.at[3])
    load_book = pltpu.make_async_copy(book_any, book_ref, load_sem.at[4])
    load_assign.start()
    load_emb.start()
    load_cent.start()
    load_codes.start()
    load_book.start()
    barrier = pltpu.get_barrier_semaphore()

    def greet(d, carry):
        pl.semaphore_signal(barrier, inc=1, device_id={"cent": lax.rem(me + d, peers)})
        return carry

    lax.fori_loop(1, peers, greet, 0)

    def each_peer(first, last, copy):
        def send(p, carry):
            copy(p, peer_of(p)).start()
            return carry

        lax.fori_loop(first, last, send, 0)

    def ids_copy(p, peer):
        return pltpu.make_async_remote_copy(
            src_ref=ids_s.at[p],
            dst_ref=ids_r.at[p],
            send_sem=ids_sem.at[0],
            recv_sem=ids_sem.at[1],
            device_id={"cent": peer},
        )

    def piece_of(k, rows, answers, at):
        c = plan[k][0]
        if c is None:
            return rows.at[at]
        return answers.at[at, :, pl.ds(c * span, span)]

    def issue(k):
        if k >= AHEAD:
            sent(k - AHEAD)

        def copy(p, peer):
            return pltpu.make_async_remote_copy(
                src_ref=piece_of(k, rows_s, ans_s, p),
                dst_ref=piece_of(k, rows_r, ans_r, p),
                send_sem=send_sem.at[k],
                recv_sem=recv_sem.at[k],
                device_id={"cent": peer},
            )

        each_peer(plan[k][1], plan[k][2], copy)

    def wait_for(piece, sem):
        pltpu.make_async_copy(piece, piece, sem).wait()

    def sent(k):
        at = pl.ds(plan[k][1], plan[k][2] - plan[k][1])
        wait_for(piece_of(k, rows_s, ans_s, at), send_sem.at[k])

    def arrived(k):
        at = pl.ds(plan[k][1], plan[k][2] - plan[k][1])
        wait_for(piece_of(k, rows_r, ans_r, at), recv_sem.at[k])

    load_assign.wait()
    a = assign_ref[...].reshape(1, num_rows)
    slot_ids = lax.broadcasted_iota(jnp.int32, (peers, num_rows), 0)
    low = jnp.bitwise_xor((slot_ids & 1) * half + (slot_ids >> 1), me) * held
    hits = ((a >= low) & (a < low + held)).astype(f32)
    before = (
        lax.broadcasted_iota(jnp.int32, (num_rows, num_rows), 0)
        < lax.broadcasted_iota(jnp.int32, (num_rows, num_rows), 1)
    ).astype(f32).astype(bf16)
    earlier = dot(hits.astype(bf16), before)
    rank = jnp.sum(earlier * hits, axis=0, keepdims=True).astype(jnp.int32)
    position = jnp.sum(slot_ids.astype(f32) * hits, axis=0, keepdims=True).astype(jnp.int32)
    labels = (hits * (a - low + 1).astype(f32)).astype(bf16)
    ranks = (lax.broadcasted_iota(jnp.int32, (LANES, num_rows), 0) == rank).astype(f32).astype(bf16)
    ids_s[...] = dot(labels, ranks, 1, 1).reshape(peers, 1, LANES)

    pl.semaphore_wait(barrier, peers - 1)
    each_peer(1, peers, ids_copy)
    ids_r[0] = ids_s[0]

    base = position * FULL + rank
    late = rank >= FULL
    targets = (
        jnp.where(late, -1, base),
        jnp.where(late, base - FULL, -1),
        jnp.where(late, base - (FULL - REST), -1),
    )
    place_ids = lax.broadcasted_iota(jnp.int32, (slots, num_rows), 0)
    for i, target in enumerate(targets):
        place_s[i] = (place_ids == target).astype(f32).astype(bf16)

    def tile(t):
        return slice(t * LANES, (t + 1) * LANES)

    def gather(choose, table, at, out, chunks):
        n = at.stop - at.start
        for c in chunks:
            for i, value in enumerate(
                (
                    dot(choose[0, at], table[:, tile(c)]),
                    dot(choose[0, at], table[:, tile(c + CHUNKS)]),
                    dot(choose[1, at], table[:, tile(c)])
                    + dot(choose[2, at], table[:, tile(c + CHUNKS)]),
                )
            ):
                out[at.start // FULL : at.stop // FULL, :, tile(3 * c + i)] = value.astype(
                    bf16
                ).reshape(n // FULL, FULL, LANES)

    load_emb.wait()
    gather(place_s, emb_ref, slice(0, slots), rows_s, range(CHUNKS))
    issue(0)

    wait_for(ids_r.at[pl.ds(1, peers - 1)], ids_sem.at[1])
    shape = (peers, FULL, LANES)
    got = jnp.broadcast_to(ids_r[...], shape)
    lane = lax.broadcasted_iota(jnp.int32, shape, 2)
    sub = lax.broadcasted_iota(jnp.int32, shape, 1)
    front = sub < REST
    first_at = jnp.where(lane == sub, got, 0.0)
    rest_at = jnp.where(lane == jnp.where(front, sub + FULL, sub + (FULL - REST)), got, 0.0)
    label_a = jnp.sum(first_at, axis=2, keepdims=True)
    label_r = jnp.sum(rest_at, axis=2, keepdims=True)
    label_b = jnp.where(front[:, :, :1], label_r, 0.0)
    label_c = jnp.where(front[:, :, :1], 0.0, label_r)
    lane_f = lane.astype(f32)
    for i, label in enumerate((label_a, label_b, label_c)):
        for h in range(held // LANES):
            pick_s[i, :, tile(h)] = (
                (label == lane_f + (1.0 + LANES * h)).astype(f32).reshape(slots, LANES).astype(bf16)
            )
    load_cent.wait()

    gather(pick_s, cent_ref, slice(0, slots), ans_s, (0,))
    issue(1)
    issue(2)
    gather(pick_s, cent_ref, slice(0, slots), ans_s, range(1, CHUNKS))
    ans_r[0] = ans_s[0]
    rows_r[0] = rows_s[0]

    load_codes.wait()
    shifted = (codes_ref[...] + 1).astype(f32).astype(bf16)
    part = subspaces // 2
    for i in range(2):
        codes_c[i, :, :part] = dot(place_s[0], shifted[i * part : (i + 1) * part], 1, 1)
    codes_c[2, :, :part] = dot(place_s[1], shifted[:part], 1, 1) + dot(
        place_s[2], shifted[part:], 1, 1
    )

    per = LANES // sub_width
    column = (lax.broadcasted_iota(jnp.int32, (slots, LANES), 1) + 1).astype(f32)
    columns = [(column + LANES * i).astype(bf16) for i in range(words // LANES)]
    kind = lax.broadcasted_iota(jnp.int32, (16, slots), 0)
    early = lax.rem(lax.broadcasted_iota(jnp.int32, (16, slots), 1), FULL) < REST
    counted = jnp.where(kind == 0, 1.0, jnp.where((kind == 1) == early, 1.0, 0.0)).astype(bf16)
    counts_t[subspaces:] = jnp.zeros_like(counts_t[subspaces:])

    def build_onehot(c):
        def build(i, carry):
            for j in range(per):
                code = jnp.broadcast_to(
                    codes_c[i, :, c * per + j : c * per + j + 1], (slots, LANES)
                ).astype(bf16)
                at = i * part + c * per + j
                for h, value in enumerate(columns):
                    onehot[at, :, tile(h)] = jnp.where(
                        code == value, jnp.ones_like(value), jnp.zeros_like(value)
                    )
            return carry

        lax.fori_loop(0, 3, build, 0)

        def count(u, carry):
            m = c * per + u
            late_counts = dot(counted, onehot[2 * part + m])
            for i in range(2):
                counts_t[pl.ds(i * part + m, 1), :] = (
                    dot(counted, onehot[i * part + m])[:1] + late_counts[1 + i : 2 + i]
                )
            return carry

        lax.fori_loop(0, per, count, 0, unroll=4)

    front_lanes = lax.rem(lax.broadcasted_iota(jnp.int32, (sub_width, slots), 1), FULL) < REST

    def sum_chunk(c):
        cut = slice(c * span, (c + 1) * span)
        res = rows_s[:, :, cut].reshape(slots, span).astype(f32) - ans_r[:, :, cut].reshape(
            slots, span
        ).astype(f32)
        res_t[...] = res.T
        res_s[:, cut] = res.astype(bf16)

        def one(u, carry):
            m = c * per + u
            at = [pl.multiple_of(i * LANES + u * sub_width, sub_width) for i in range(3)]
            main = [res_t[pl.ds(at[i], sub_width), :].astype(bf16) for i in range(2)]
            beside = res_t[pl.ds(at[2], sub_width), :]
            both = jnp.concatenate(
                [jnp.where(front_lanes, beside, 0.0), jnp.where(front_lanes, 0.0, beside)], axis=0
            ).astype(bf16)
            late_sums = dot(both, onehot[2 * part + m])
            for i in range(2):
                sums_t[pl.ds(at[i], sub_width), :] = (
                    dot(main[i], onehot[i * part + m])
                    + late_sums[i * sub_width : (i + 1) * sub_width]
                )
            return carry

        lax.fori_loop(0, per, one, 0, unroll=8)

    cuts = [(2 * c + (c > 1), 2 * c + 2 + (c >= 1)) for c in range(CHUNKS)]
    order = []
    for c in range(CHUNKS):
        order += [c, c + CHUNKS] + ([tiles] if c == 1 else [])

    def pair_copy(c):
        at = pl.ds(cuts[c][0], cuts[c][1] - cuts[c][0])
        return pltpu.make_async_remote_copy(
            src_ref=pair_s.at[1 - core, at],
            dst_ref=pair_r.at[at],
            send_sem=pair_send.at[c],
            recv_sem=pair_recv.at[c],
            device_id={"cent": away(1)},
        )

    def put(c):
        for k in range(*cuts[c]):
            t = order[k]
            value = (counts_t[...] if t == tiles else sums_t[tile(t // CHUNKS), :]).T
            if mine % 8 == 0:
                split = value.reshape(outer, INNER, 2, mine, LANES)
                for b in range(2):
                    for i in range(INNER):
                        pair_s[b, k, i] = split[:, i, b]
            else:
                for p in range(peers):
                    pair_s[p % 2, k, p // 2 % INNER, p // 2 // INNER] = value[
                        p * mine : (p + 1) * mine
                    ]
        pair_copy(c).start()

    def hops(src, dst, sems, c, count, stride, place):
        at = pl.ds(cuts[c][0], cuts[c][1] - cuts[c][0])
        for e in range(1, count):
            peer = away(stride * e)
            pltpu.make_async_remote_copy(
                src_ref=src.at[place(peer), at],
                dst_ref=dst.at[e - 1, at],
                send_sem=sems[0].at[c],
                recv_sem=sems[1].at[c],
                device_id={"cent": peer},
            ).start()

    def hops_wait(dst, sem, c, count):
        at = pl.ds(cuts[c][0], cuts[c][1] - cuts[c][0])
        wait_for(dst.at[pl.ds(0, count - 1), at], sem.at[c])

    def inner_of(peer):
        return lax.rem(lax.div(peer, 2), INNER)

    def outer_of(peer):
        return lax.div(peer, 2 * INNER)

    def add_pair(c):
        pair_copy(c).wait_recv()
        for k in range(*cuts[c]):
            plane_s[:, k] = pair_s[core, k] + pair_r[k]
        if c not in DIRECT:
            hops(plane_s, plane_r, (plane_send, plane_recv), c, INNER, 2, inner_of)
            return
        at = pl.ds(cuts[c][0], cuts[c][1] - cuts[c][0])
        for d in range(1, half):
            peer = away(2 * d)
            pltpu.make_async_remote_copy(
                src_ref=plane_s.at[inner_of(peer), at, outer_of(peer)],
                dst_ref=direct_r.at[d - 1, at],
                send_sem=plane_send.at[c],
                recv_sem=plane_recv.at[c],
                device_id={"cent": peer},
            ).start()

    def direct_copy(c, sending):
        piece = direct_r.at[:, pl.ds(cuts[c][0], cuts[c][1] - cuts[c][0])]
        sem = plane_send.at[c] if sending else plane_recv.at[c]
        return pltpu.make_async_copy(piece, piece, sem)

    def add_plane(c):
        if c in DIRECT:
            return
        first, last = cuts[c]
        hops_wait(plane_r, plane_recv, c, INNER)
        total = plane_s[inner_of(me), first:last]
        for e in range(1, INNER):
            total = total + plane_r[e - 1, first:last]
        for o in range(outer):
            line_s[o, first:last] = total[:, o]
        hops(line_s, line_r, (line_send, line_recv), c, outer, 2 * INNER, outer_of)

    ones = jnp.ones((slots, LANES), bf16)
    tail = slice(plan[-1][1] * FULL, slots)
    lead = slice(0, plan[-1][1] * FULL)

    issue(3)
    issue(4)
    issue(5)
    issue(6)
    issue(7)
    issue(8)
    issue(9)
    build_onehot(0)
    build_onehot(1)
    build_onehot(2)
    arrived(1)
    arrived(2)
    sum_chunk(0)
    put(0)
    add_pair(0)
    weights = dot(pick_s[0], ones, 0, 0) + dot(pick_s[1], ones, 0, 0) + prior_weight
    inverse = 1.0 / weights
    for i in range(2):
        pick_t[i] = jnp.concatenate([pick_s[0, tail], pick_s[1 + i, tail]], axis=0).T
    arrived(3)
    arrived(4)
    sum_chunk(1)
    put(1)
    add_pair(1)
    add_plane(0)
    arrived(5)
    arrived(6)
    sum_chunk(2)
    put(2)
    add_pair(2)
    add_plane(1)
    for c in range(CHUNKS):
        for i in range(2):
            resid_ref[:, tile(c + CHUNKS * i)] = (
                dot(place_s[0], res_s[:, tile(3 * c + i)], 0, 0)
                + dot(place_s[1 + i], res_s[:, tile(3 * c + 2)], 0, 0)
            ).astype(bf16)
    add_plane(2)

    def coarse(at, choose):
        out = []
        for i in range(2):
            for c in range(CHUNKS):
                main = rows_r[at.start // FULL : at.stop // FULL, :, tile(3 * c + i)]
                rest = rows_r[at.start // FULL : at.stop // FULL, :, tile(3 * c + 2)]
                n = at.stop - at.start
                out.append((tile(c + CHUNKS * i), choose(i, main.reshape(n, LANES), rest.reshape(n, LANES))))
        return out

    arrived(0)
    arrived(7)
    arrived(8)
    for cols, value in coarse(
        lead,
        lambda i, main, rest: dot(pick_s[0, lead], main, 0, 0) + dot(pick_s[1 + i, lead], rest, 0, 0),
    ):
        base_s[:, cols] = value + prior_weight * cent_ref[:, cols].astype(f32)
    load_book.wait()
    col = lax.broadcasted_iota(jnp.int32, (LANES, width), 1)
    row = lax.broadcasted_iota(jnp.int32, (LANES, width), 0) * sub_width
    expand = ((col >= row) & (col < row + sub_width)).astype(f32)
    own = [None] * (tiles + 1)
    for c in range(CHUNKS):
        if c in DIRECT:
            direct_copy(c, 0).wait()
            for k in range(*cuts[c]):
                own[order[k]] = plane_s[inner_of(me), k, outer_of(me)] + jnp.sum(direct_r[:, k], axis=0)
        else:
            hops_wait(line_r, line_recv, c, outer)
            for k in range(*cuts[c]):
                own[order[k]] = line_s[outer_of(me), k] + jnp.sum(line_r[:, k], axis=0)
    spread = dot(own[tiles], expand, precision=lax.Precision.HIGHEST)
    for t in range(tiles):
        newb_ref[:, tile(t)] = (own[t] + prior_weight * book_ref[:, tile(t)]) / (
            spread[:, tile(t)] + prior_weight
        )

    arrived(9)
    for cols, value in coarse(
        tail, lambda i, main, rest: dot(pick_t[i], jnp.concatenate([main, rest], axis=0))
    ):
        newc_ref[:, cols] = (value + base_s[:, cols]) * inverse

    wait_for(ids_s.at[pl.ds(1, peers - 1)], ids_sem.at[0])
    for k in range(len(plan) - AHEAD, len(plan)):
        sent(k)
    for c in range(CHUNKS):
        pair_copy(c).wait_send()
        if c in DIRECT:
            direct_copy(c, 1).wait()
        else:
            hops_wait(plane_r, plane_send, c, INNER)
            hops_wait(line_r, line_send, c, outer)


def store_kernel(*refs):
    copies = [
        pltpu.make_async_copy(refs[i], refs[3 + i], refs[6].at[i]) for i in range(3)
    ]
    for copy in copies:
        copy.start()
    for copy in copies:
        copy.wait()


def shards(embeddings, assign, codes, centroids, codebook):
    num_rows, width = embeddings.shape
    held = centroids.shape[0]
    mine = codebook.shape[0]
    subspaces = codes.shape[1]
    peers = lax.axis_size("cent")
    slots = peers * FULL
    words = mine * peers
    outer = peers // 2 // INNER
    long = width + width // 2
    tiles = width // LANES + 1
    plan = send_plan(peers)
    last = (peers - plan[-1][1]) * FULL
    hbm = pl.BlockSpec(memory_space=pltpu.HBM)
    vmem = pl.BlockSpec(memory_space=pltpu.VMEM)
    outs = (
        jax.ShapeDtypeStruct((num_rows, width), bf16),
        jax.ShapeDtypeStruct((held, width), f32),
        jax.ShapeDtypeStruct((mine, width), f32),
    )
    made = pl.pallas_call(
        functools.partial(step_kernel, peers),
        out_shape=tuple(pltpu.VMEM(out.shape, out.dtype) for out in outs),
        in_specs=[hbm] * 5,
        out_specs=(vmem,) * 3,
        scratch_shapes=[
            pltpu.VMEM((peers, 1, LANES), f32),
            pltpu.VMEM((peers, 1, LANES), f32),
            pltpu.VMEM((peers, FULL, long), bf16),
            pltpu.VMEM((peers, FULL, long), bf16),
            pltpu.VMEM((peers, FULL, long), bf16),
            pltpu.VMEM((peers, FULL, long), bf16),
            pltpu.VMEM((2, tiles, INNER, outer, mine, LANES), f32),
            pltpu.VMEM((tiles, INNER, outer, mine, LANES), f32),
            pltpu.VMEM((INNER, tiles, outer, mine, LANES), f32),
            pltpu.VMEM((INNER - 1, tiles, outer, mine, LANES), f32),
            pltpu.VMEM((outer, tiles, mine, LANES), f32),
            pltpu.VMEM((outer - 1, tiles, mine, LANES), f32),
            pltpu.VMEM((peers // 2 - 1, tiles, mine, LANES), f32),
            pltpu.VMEM((3, slots, num_rows), bf16),
            pltpu.VMEM((3, slots, held), bf16),
            pltpu.VMEM((2, held, 2 * last), bf16),
            pltpu.VMEM((3, slots, LANES), f32),
            pltpu.VMEM((subspaces * 3 // 2, slots, words), bf16),
            pltpu.VMEM((slots, long), bf16),
            pltpu.VMEM((3 * LANES, slots), f32),
            pltpu.VMEM((2 * LANES, words), f32),
            pltpu.VMEM((LANES, words), f32),
            pltpu.VMEM((held, width), f32),
            pltpu.VMEM((num_rows, width), bf16),
            pltpu.VMEM((held, width), bf16),
            pltpu.VMEM((num_rows,), jnp.int32),
            pltpu.VMEM((subspaces, num_rows), jnp.int32),
            pltpu.VMEM((mine, width), f32),
            pltpu.SemaphoreType.DMA((5,)),
            pltpu.SemaphoreType.DMA((2,)),
            pltpu.SemaphoreType.DMA((len(plan),)),
            pltpu.SemaphoreType.DMA((len(plan),)),
        ]
        + [pltpu.SemaphoreType.DMA((CHUNKS,))] * 6,
        compiler_params=pltpu.CompilerParams(
            collective_id=0, has_side_effects=True, vmem_limit_bytes=56 * 1024 * 1024
        ),
    )(
        *(
            pltpu.with_memory_space_constraint(x, pltpu.HBM)
            for x in (assign, embeddings, codes.T, centroids, codebook)
        )
    )
    return pl.pallas_call(
        store_kernel,
        out_shape=outs,
        in_specs=[vmem] * 3,
        out_specs=(hbm,) * 3,
        scratch_shapes=[pltpu.SemaphoreType.DMA((3,))],
    )(*(pltpu.with_memory_space_constraint(x, pltpu.VMEM) for x in made))


def solution(mesh):
    spec = P(("group", "cent"), None)
    in_specs = (spec, P(("group", "cent")), spec, spec, spec)
    return jax.shard_map(
        shards, mesh=mesh, in_specs=in_specs, out_specs=(spec, spec, spec), check_vma=False
    )
```

```python
import functools

import jax
import jax.numpy as jnp
from jax import lax
from jax.experimental import pallas as pl
from jax.experimental.pallas import tpu as pltpu
from jax.sharding import PartitionSpec as P

CAP = 12
FULL = 8
REST = CAP - FULL
LANES = 128
INNER = 4
CHUNKS = 3
DIRECT = (2,)
AHEAD = 10

prior_weight = 16.0
f32 = jnp.float32
bf16 = jnp.bfloat16


def dot(a, b, ca=1, cb=0, **kw):
    return lax.dot_general(
        a, b, (((ca,), (cb,)), ((), ())), preferred_element_type=f32, **kw
    )


def send_plan(peers):
    eighth = peers // 8
    cuts = [(1, 4 * eighth), (4 * eighth, peers)]
    rows = [(1, 2 * eighth), (2 * eighth, 4 * eighth), (4 * eighth, 7 * eighth), (7 * eighth, peers)]
    plan = [(None,) + cut for cut in rows[:1]]
    for c in range(CHUNKS):
        plan += [(c,) + cut for cut in cuts]
    return plan + [(None,) + cut for cut in rows[1:]]


def step_kernel(
    peers,
    assign_any,
    emb_any,
    codes_any,
    cent_any,
    book_any,
    resid_ref,
    newc_ref,
    newb_ref,
    ids_s,
    ids_r,
    ans_s,
    ans_r,
    rows_s,
    rows_r,
    pair_s,
    pair_r,
    plane_s,
    plane_r,
    line_s,
    line_r,
    direct_r,
    place_s,
    pick_s,
    pick_t,
    codes_c,
    onehot,
    res_s,
    res_t,
    sums_t,
    counts_t,
    base_s,
    emb_ref,
    cent_ref,
    assign_ref,
    codes_ref,
    book_ref,
    load_sem,
    ids_sem,
    send_sem,
    recv_sem,
    pair_send,
    pair_recv,
    plane_send,
    plane_recv,
    line_send,
    line_recv,
):
    me = lax.axis_index("cent")
    num_rows, width = emb_ref.shape
    side = width // 2
    subspaces = codes_ref.shape[0]
    sub_width = width // subspaces
    held = cent_ref.shape[0]
    mine = book_ref.shape[0]
    words = mine * peers
    slots = peers * FULL
    half = peers // 2
    core = lax.rem(me, 2)
    outer = peers // 2 // INNER
    tiles = width // LANES
    bits = peers.bit_length() - 1
    span = 3 * LANES
    plan = send_plan(peers)

    move = [(1 - 2 * lax.rem(lax.div(me, 1 << i), 2)) * (1 << i) for i in range(bits)]
    turn = [move[-1]] + move[:-1]

    def peer_of(p):
        peer = me
        for i in range(bits):
            peer = peer + lax.rem(lax.div(p, 1 << i), 2) * turn[i]
        return peer

    def away(d):
        return me + sum(move[i] for i in range(bits) if d >> i & 1)

    load_assign = pltpu.make_async_copy(assign_any, assign_ref, load_sem.at[0])
    load_emb = pltpu.make_async_copy(emb_any, emb_ref, load_sem.at[1])
    load_cent = pltpu.make_async_copy(cent_any, cent_ref, load_sem.at[2])
    load_codes = pltpu.make_async_copy(codes_any, codes_ref, load_sem.at[3])
    load_book = pltpu.make_async_copy(book_any, book_ref, load_sem.at[4])
    load_assign.start()
    load_emb.start()
    load_cent.start()
    load_codes.start()
    load_book.start()
    barrier = pltpu.get_barrier_semaphore()

    def greet(d, carry):
        pl.semaphore_signal(barrier, inc=1, device_id={"cent": lax.rem(me + d, peers)})
        return carry

    lax.fori_loop(1, peers, greet, 0)

    def each_peer(first, last, copy):
        def send(p, carry):
            copy(p, peer_of(p)).start()
            return carry

        lax.fori_loop(first, last, send, 0)

    def ids_copy(p, peer):
        return pltpu.make_async_remote_copy(
            src_ref=ids_s.at[p],
            dst_ref=ids_r.at[p],
            send_sem=ids_sem.at[0],
            recv_sem=ids_sem.at[1],
            device_id={"cent": peer},
        )

    def piece_of(k, rows, answers, at):
        c = plan[k][0]
        if c is None:
            return rows.at[at]
        return answers.at[at, :, pl.ds(c * span, span)]

    def issue(k):
        if k >= AHEAD:
            sent(k - AHEAD)

        def copy(p, peer):
            return pltpu.make_async_remote_copy(
                src_ref=piece_of(k, rows_s, ans_s, p),
                dst_ref=piece_of(k, rows_r, ans_r, p),
                send_sem=send_sem.at[k],
                recv_sem=recv_sem.at[k],
                device_id={"cent": peer},
            )

        each_peer(plan[k][1], plan[k][2], copy)

    def wait_for(piece, sem):
        pltpu.make_async_copy(piece, piece, sem).wait()

    def sent(k):
        at = pl.ds(plan[k][1], plan[k][2] - plan[k][1])
        wait_for(piece_of(k, rows_s, ans_s, at), send_sem.at[k])

    def arrived(k):
        at = pl.ds(plan[k][1], plan[k][2] - plan[k][1])
        wait_for(piece_of(k, rows_r, ans_r, at), recv_sem.at[k])

    load_assign.wait()
    a = assign_ref[...].reshape(1, num_rows)
    slot_ids = lax.broadcasted_iota(jnp.int32, (peers, num_rows), 0)
    low = jnp.bitwise_xor((slot_ids & 1) * half + (slot_ids >> 1), me) * held
    hits = ((a >= low) & (a < low + held)).astype(f32)
    before = (
        lax.broadcasted_iota(jnp.int32, (num_rows, num_rows), 0)
        < lax.broadcasted_iota(jnp.int32, (num_rows, num_rows), 1)
    ).astype(f32).astype(bf16)
    earlier = dot(hits.astype(bf16), before)
    rank = jnp.sum(earlier * hits, axis=0, keepdims=True).astype(jnp.int32)
    position = jnp.sum(slot_ids.astype(f32) * hits, axis=0, keepdims=True).astype(jnp.int32)
    labels = (hits * (a - low + 1).astype(f32)).astype(bf16)
    ranks = (lax.broadcasted_iota(jnp.int32, (LANES, num_rows), 0) == rank).astype(f32).astype(bf16)
    ids_s[...] = dot(labels, ranks, 1, 1).reshape(peers, 1, LANES)

    pl.semaphore_wait(barrier, peers - 1)
    each_peer(1, peers, ids_copy)
    ids_r[0] = ids_s[0]

    base = position * FULL + rank
    late = rank >= FULL
    targets = (
        jnp.where(late, -1, base),
        jnp.where(late, base - FULL, -1),
        jnp.where(late, base - (FULL - REST), -1),
    )
    place_ids = lax.broadcasted_iota(jnp.int32, (slots, num_rows), 0)
    for i, target in enumerate(targets):
        place_s[i] = (place_ids == target).astype(f32).astype(bf16)

    def tile(t):
        return slice(t * LANES, (t + 1) * LANES)

    def gather(choose, table, at, out, chunks):
        n = at.stop - at.start
        for c in chunks:
            for i, value in enumerate(
                (
                    dot(choose[0, at], table[:, tile(c)]),
                    dot(choose[0, at], table[:, tile(c + CHUNKS)]),
                    dot(choose[1, at], table[:, tile(c)])
                    + dot(choose[2, at], table[:, tile(c + CHUNKS)]),
                )
            ):
                out[at.start // FULL : at.stop // FULL, :, tile(3 * c + i)] = value.astype(
                    bf16
                ).reshape(n // FULL, FULL, LANES)

    load_emb.wait()
    gather(place_s, emb_ref, slice(0, slots), rows_s, range(CHUNKS))
    issue(0)

    wait_for(ids_r.at[pl.ds(1, peers - 1)], ids_sem.at[1])
    shape = (peers, FULL, LANES)
    got = jnp.broadcast_to(ids_r[...], shape)
    lane = lax.broadcasted_iota(jnp.int32, shape, 2)
    sub = lax.broadcasted_iota(jnp.int32, shape, 1)
    front = sub < REST
    first_at = jnp.where(lane == sub, got, 0.0)
    rest_at = jnp.where(lane == jnp.where(front, sub + FULL, sub + (FULL - REST)), got, 0.0)
    label_a = jnp.sum(first_at, axis=2, keepdims=True)
    label_r = jnp.sum(rest_at, axis=2, keepdims=True)
    label_b = jnp.where(front[:, :, :1], label_r, 0.0)
    label_c = jnp.where(front[:, :, :1], 0.0, label_r)
    lane_f = lane.astype(f32)
    for i, label in enumerate((label_a, label_b, label_c)):
        for h in range(held // LANES):
            pick_s[i, :, tile(h)] = (
                (label == lane_f + (1.0 + LANES * h)).astype(f32).reshape(slots, LANES).astype(bf16)
            )
    load_cent.wait()

    gather(pick_s, cent_ref, slice(0, slots), ans_s, (0,))
    issue(1)
    issue(2)
    gather(pick_s, cent_ref, slice(0, slots), ans_s, range(1, CHUNKS))
    ans_r[0] = ans_s[0]
    rows_r[0] = rows_s[0]

    load_codes.wait()
    shifted = (codes_ref[...] + 1).astype(f32).astype(bf16)
    part = subspaces // 2
    for i in range(2):
        codes_c[i, :, :part] = dot(place_s[0], shifted[i * part : (i + 1) * part], 1, 1)
    codes_c[2, :, :part] = dot(place_s[1], shifted[:part], 1, 1) + dot(
        place_s[2], shifted[part:], 1, 1
    )

    per = LANES // sub_width
    column = (lax.broadcasted_iota(jnp.int32, (slots, LANES), 1) + 1).astype(f32)
    columns = [(column + LANES * i).astype(bf16) for i in range(words // LANES)]
    kind = lax.broadcasted_iota(jnp.int32, (16, slots), 0)
    early = lax.rem(lax.broadcasted_iota(jnp.int32, (16, slots), 1), FULL) < REST
    counted = jnp.where(kind == 0, 1.0, jnp.where((kind == 1) == early, 1.0, 0.0)).astype(bf16)
    counts_t[subspaces:] = jnp.zeros_like(counts_t[subspaces:])

    def build_onehot(c):
        def build(i, carry):
            for j in range(per):
                code = jnp.broadcast_to(
                    codes_c[i, :, c * per + j : c * per + j + 1], (slots, LANES)
                ).astype(bf16)
                at = i * part + c * per + j
                for h, value in enumerate(columns):
                    onehot[at, :, tile(h)] = jnp.where(
                        code == value, jnp.ones_like(value), jnp.zeros_like(value)
                    )
            return carry

        lax.fori_loop(0, 3, build, 0)

        def count(u, carry):
            m = c * per + u
            late_counts = dot(counted, onehot[2 * part + m])
            for i in range(2):
                counts_t[pl.ds(i * part + m, 1), :] = (
                    dot(counted, onehot[i * part + m])[:1] + late_counts[1 + i : 2 + i]
                )
            return carry

        lax.fori_loop(0, per, count, 0, unroll=4)

    front_lanes = lax.rem(lax.broadcasted_iota(jnp.int32, (sub_width, slots), 1), FULL) < REST

    def sum_chunk(c):
        cut = slice(c * span, (c + 1) * span)
        res = rows_s[:, :, cut].reshape(slots, span).astype(f32) - ans_r[:, :, cut].reshape(
            slots, span
        ).astype(f32)
        res_t[...] = res.T
        res_s[:, cut] = res.astype(bf16)

        def one(u, carry):
            m = c * per + u
            at = [pl.multiple_of(i * LANES + u * sub_width, sub_width) for i in range(3)]
            main = [res_t[pl.ds(at[i], sub_width), :].astype(bf16) for i in range(2)]
            beside = res_t[pl.ds(at[2], sub_width), :]
            both = jnp.concatenate(
                [jnp.where(front_lanes, beside, 0.0), jnp.where(front_lanes, 0.0, beside)], axis=0
            ).astype(bf16)
            late_sums = dot(both, onehot[2 * part + m])
            for i in range(2):
                sums_t[pl.ds(at[i], sub_width), :] = (
                    dot(main[i], onehot[i * part + m])
                    + late_sums[i * sub_width : (i + 1) * sub_width]
                )
            return carry

        lax.fori_loop(0, per, one, 0, unroll=8)

    cuts = [(2 * c + (c > 1), 2 * c + 2 + (c >= 1)) for c in range(CHUNKS)]
    order = []
    for c in range(CHUNKS):
        order += [c, c + CHUNKS] + ([tiles] if c == 1 else [])

    def pair_copy(c):
        at = pl.ds(cuts[c][0], cuts[c][1] - cuts[c][0])
        return pltpu.make_async_remote_copy(
            src_ref=pair_s.at[1 - core, at],
            dst_ref=pair_r.at[at],
            send_sem=pair_send.at[c],
            recv_sem=pair_recv.at[c],
            device_id={"cent": away(1)},
        )

    def put(c):
        for k in range(*cuts[c]):
            t = order[k]
            value = (counts_t[...] if t == tiles else sums_t[tile(t // CHUNKS), :]).T
            if mine % 8 == 0:
                split = value.reshape(outer, INNER, 2, mine, LANES)
                for b in range(2):
                    for i in range(INNER):
                        pair_s[b, k, i] = split[:, i, b]
            else:
                for p in range(peers):
                    pair_s[p % 2, k, p // 2 % INNER, p // 2 // INNER] = value[
                        p * mine : (p + 1) * mine
                    ]
        pair_copy(c).start()

    def hops(src, dst, sems, c, count, stride, place):
        at = pl.ds(cuts[c][0], cuts[c][1] - cuts[c][0])
        for e in range(1, count):
            peer = away(stride * e)
            pltpu.make_async_remote_copy(
                src_ref=src.at[place(peer), at],
                dst_ref=dst.at[e - 1, at],
                send_sem=sems[0].at[c],
                recv_sem=sems[1].at[c],
                device_id={"cent": peer},
            ).start()

    def hops_wait(dst, sem, c, count):
        at = pl.ds(cuts[c][0], cuts[c][1] - cuts[c][0])
        wait_for(dst.at[pl.ds(0, count - 1), at], sem.at[c])

    def inner_of(peer):
        return lax.rem(lax.div(peer, 2), INNER)

    def outer_of(peer):
        return lax.div(peer, 2 * INNER)

    def add_pair(c):
        pair_copy(c).wait_recv()
        for k in range(*cuts[c]):
            plane_s[:, k] = pair_s[core, k] + pair_r[k]
        if c not in DIRECT:
            hops(plane_s, plane_r, (plane_send, plane_recv), c, INNER, 2, inner_of)
            return
        at = pl.ds(cuts[c][0], cuts[c][1] - cuts[c][0])
        for d in range(1, half):
            peer = away(2 * d)
            pltpu.make_async_remote_copy(
                src_ref=plane_s.at[inner_of(peer), at, outer_of(peer)],
                dst_ref=direct_r.at[d - 1, at],
                send_sem=plane_send.at[c],
                recv_sem=plane_recv.at[c],
                device_id={"cent": peer},
            ).start()

    def direct_copy(c, sending):
        piece = direct_r.at[:, pl.ds(cuts[c][0], cuts[c][1] - cuts[c][0])]
        sem = plane_send.at[c] if sending else plane_recv.at[c]
        return pltpu.make_async_copy(piece, piece, sem)

    def add_plane(c):
        if c in DIRECT:
            return
        first, last = cuts[c]
        hops_wait(plane_r, plane_recv, c, INNER)
        total = plane_s[inner_of(me), first:last]
        for e in range(1, INNER):
            total = total + plane_r[e - 1, first:last]
        for o in range(outer):
            line_s[o, first:last] = total[:, o]
        hops(line_s, line_r, (line_send, line_recv), c, outer, 2 * INNER, outer_of)

    ones = jnp.ones((slots, LANES), bf16)
    tail = slice(plan[-1][1] * FULL, slots)
    lead = slice(0, plan[-1][1] * FULL)

    issue(3)
    issue(4)
    issue(5)
    issue(6)
    issue(7)
    build_onehot(0)
    issue(8)
    build_onehot(1)
    issue(9)
    build_onehot(2)
    arrived(1)
    arrived(2)
    sum_chunk(0)
    put(0)
    add_pair(0)
    weights = dot(pick_s[0], ones, 0, 0) + dot(pick_s[1], ones, 0, 0) + prior_weight
    inverse = 1.0 / weights
    for i in range(2):
        pick_t[i] = jnp.concatenate([pick_s[0, tail], pick_s[1 + i, tail]], axis=0).T
    arrived(3)
    arrived(4)
    sum_chunk(1)
    put(1)
    add_pair(1)
    add_plane(0)
    arrived(5)
    arrived(6)
    sum_chunk(2)
    put(2)
    add_pair(2)
    add_plane(1)
    for c in range(CHUNKS):
        for i in range(2):
            resid_ref[:, tile(c + CHUNKS * i)] = (
                dot(place_s[0], res_s[:, tile(3 * c + i)], 0, 0)
                + dot(place_s[1 + i], res_s[:, tile(3 * c + 2)], 0, 0)
            ).astype(bf16)
    add_plane(2)

    def coarse(at, choose):
        out = []
        for i in range(2):
            for c in range(CHUNKS):
                main = rows_r[at.start // FULL : at.stop // FULL, :, tile(3 * c + i)]
                rest = rows_r[at.start // FULL : at.stop // FULL, :, tile(3 * c + 2)]
                n = at.stop - at.start
                out.append((tile(c + CHUNKS * i), choose(i, main.reshape(n, LANES), rest.reshape(n, LANES))))
        return out

    arrived(0)
    arrived(7)
    arrived(8)
    for cols, value in coarse(
        lead,
        lambda i, main, rest: dot(pick_s[0, lead], main, 0, 0) + dot(pick_s[1 + i, lead], rest, 0, 0),
    ):
        base_s[:, cols] = value + prior_weight * cent_ref[:, cols].astype(f32)
    load_book.wait()
    col = lax.broadcasted_iota(jnp.int32, (LANES, width), 1)
    row = lax.broadcasted_iota(jnp.int32, (LANES, width), 0) * sub_width
    expand = ((col >= row) & (col < row + sub_width)).astype(f32)
    own = [None] * (tiles + 1)

    def gather_sums(c):
        if c in DIRECT:
            direct_copy(c, 0).wait()
        else:
            hops_wait(line_r, line_recv, c, outer)
        for k in range(*cuts[c]):
            if c in DIRECT:
                first = plane_s[inner_of(me), k, outer_of(me)]
                own[order[k]] = first + jnp.sum(direct_r[:, k], axis=0)
            else:
                own[order[k]] = line_s[outer_of(me), k] + jnp.sum(line_r[:, k], axis=0)

    def store_book(c, divisor):
        for t in (c, c + CHUNKS):
            newb_ref[:, tile(t)] = (own[t] + prior_weight * book_ref[:, tile(t)]) / divisor[
                :, tile(t)
            ]

    gather_sums(0)
    gather_sums(1)
    divisor = dot(own[tiles], expand, precision=lax.Precision.HIGHEST) + prior_weight
    store_book(0, divisor)
    store_book(1, divisor)

    arrived(9)
    for cols, value in coarse(
        tail, lambda i, main, rest: dot(pick_t[i], jnp.concatenate([main, rest], axis=0))
    ):
        newc_ref[:, cols] = (value + base_s[:, cols]) * inverse
    gather_sums(2)
    store_book(2, divisor)

    wait_for(ids_s.at[pl.ds(1, peers - 1)], ids_sem.at[0])
    for k in range(len(plan) - AHEAD, len(plan)):
        sent(k)
    for c in range(CHUNKS):
        pair_copy(c).wait_send()
        if c in DIRECT:
            direct_copy(c, 1).wait()
        else:
            hops_wait(plane_r, plane_send, c, INNER)
            hops_wait(line_r, line_send, c, outer)


def store_kernel(*refs):
    copies = [
        pltpu.make_async_copy(refs[i], refs[3 + i], refs[6].at[i]) for i in range(3)
    ]
    for copy in copies:
        copy.start()
    for copy in copies:
        copy.wait()


def shards(embeddings, assign, codes, centroids, codebook):
    num_rows, width = embeddings.shape
    held = centroids.shape[0]
    mine = codebook.shape[0]
    subspaces = codes.shape[1]
    peers = lax.axis_size("cent")
    slots = peers * FULL
    words = mine * peers
    outer = peers // 2 // INNER
    long = width + width // 2
    tiles = width // LANES + 1
    plan = send_plan(peers)
    last = (peers - plan[-1][1]) * FULL
    hbm = pl.BlockSpec(memory_space=pltpu.HBM)
    vmem = pl.BlockSpec(memory_space=pltpu.VMEM)
    outs = (
        jax.ShapeDtypeStruct((num_rows, width), bf16),
        jax.ShapeDtypeStruct((held, width), f32),
        jax.ShapeDtypeStruct((mine, width), f32),
    )
    made = pl.pallas_call(
        functools.partial(step_kernel, peers),
        out_shape=tuple(pltpu.VMEM(out.shape, out.dtype) for out in outs),
        in_specs=[hbm] * 5,
        out_specs=(vmem,) * 3,
        scratch_shapes=[
            pltpu.VMEM((peers, 1, LANES), f32),
            pltpu.VMEM((peers, 1, LANES), f32),
            pltpu.VMEM((peers, FULL, long), bf16),
            pltpu.VMEM((peers, FULL, long), bf16),
            pltpu.VMEM((peers, FULL, long), bf16),
            pltpu.VMEM((peers, FULL, long), bf16),
            pltpu.VMEM((2, tiles, INNER, outer, mine, LANES), f32),
            pltpu.VMEM((tiles, INNER, outer, mine, LANES), f32),
            pltpu.VMEM((INNER, tiles, outer, mine, LANES), f32),
            pltpu.VMEM((INNER - 1, tiles, outer, mine, LANES), f32),
            pltpu.VMEM((outer, tiles, mine, LANES), f32),
            pltpu.VMEM((outer - 1, tiles, mine, LANES), f32),
            pltpu.VMEM((peers // 2 - 1, tiles, mine, LANES), f32),
            pltpu.VMEM((3, slots, num_rows), bf16),
            pltpu.VMEM((3, slots, held), bf16),
            pltpu.VMEM((2, held, 2 * last), bf16),
            pltpu.VMEM((3, slots, LANES), f32),
            pltpu.VMEM((subspaces * 3 // 2, slots, words), bf16),
            pltpu.VMEM((slots, long), bf16),
            pltpu.VMEM((3 * LANES, slots), f32),
            pltpu.VMEM((2 * LANES, words), f32),
            pltpu.VMEM((LANES, words), f32),
            pltpu.VMEM((held, width), f32),
            pltpu.VMEM((num_rows, width), bf16),
            pltpu.VMEM((held, width), bf16),
            pltpu.VMEM((num_rows,), jnp.int32),
            pltpu.VMEM((subspaces, num_rows), jnp.int32),
            pltpu.VMEM((mine, width), f32),
            pltpu.SemaphoreType.DMA((5,)),
            pltpu.SemaphoreType.DMA((2,)),
            pltpu.SemaphoreType.DMA((len(plan),)),
            pltpu.SemaphoreType.DMA((len(plan),)),
        ]
        + [pltpu.SemaphoreType.DMA((CHUNKS,))] * 6,
        compiler_params=pltpu.CompilerParams(
            collective_id=0, has_side_effects=True, vmem_limit_bytes=56 * 1024 * 1024
        ),
    )(
        *(
            pltpu.with_memory_space_constraint(x, pltpu.HBM)
            for x in (assign, embeddings, codes.T, centroids, codebook)
        )
    )
    return pl.pallas_call(
        store_kernel,
        out_shape=outs,
        in_specs=[vmem] * 3,
        out_specs=(hbm,) * 3,
        scratch_shapes=[pltpu.SemaphoreType.DMA((3,))],
    )(*(pltpu.with_memory_space_constraint(x, pltpu.VMEM) for x in made))


def solution(mesh):
    spec = P(("group", "cent"), None)
    in_specs = (spec, P(("group", "cent")), spec, spec, spec)
    return jax.shard_map(
        shards, mesh=mesh, in_specs=in_specs, out_specs=(spec, spec, spec), check_vma=False
    )
```
